32 devices in a mesh: tier: 8 (over z, y), mat: 4 (over x, core).
Axes of the slice: x: 2, y: 2, z: 4, core: 2. Of those that a mesh axis runs over, the one named last changes fastest.
Arguments:
- costate: bfloat16 [128, 2, 256, 256], P(('tier', 'mat')), may hold values from -6 to 6
- hamiltonian: bfloat16 [256, 256], replicated, may hold values from -0.375 to 0.375
- couplers: bfloat16 [3, 256, 256], replicated, may hold values from -0.375 to 0.375
- damping: float32 [12], replicated, may hold values from 0.05 to 0.5
- coupling: float32 [2, 12], replicated, may hold values from -0.9 to 0.9
- levels: int32 [128, 12], P(('tier', 'mat')), may hold values from 0 to 3
- neighbour_slot: int32 [128, 24], P(('tier', 'mat')), may hold values from 0 to 15
- neighbour_mode: int32 [128, 24], P(('tier', 'mat')), may hold values from 0 to 11
- neighbour_flag: int32 [128, 24], P(('tier', 'mat')), may hold values from -1 to 1
- send_index: int32 [32, 16], P(('tier', 'mat')), may hold values from 0 to 3
Outputs:
- increment: float32 [128, 2, 256, 256], P(('tier', 'mat'))
- bath_gradient: float32 [12], replicated
The draws below stay inside these ranges and needn't reach their ends.
All inputs are finite; a program needn't handle non-finite values.
Results may differ from the reference program's by a relative error of at most 0.0053.
Values may be sent and summed in bfloat16 or wider, within the bound.
A program may use at most 128 MiB of HBM per device.

```python
import math
import jax
import jax.numpy as jnp
from jax import lax

NL = 256
MODES = 12
OPS = 3
NEIGH = 24
CAP = 2
MB_DEV = 4
BLOCKS = 32
ADOS = 128
SLOTS = 16
N_MAT = 4


def set_ends(array, key, low, high):
    extent = array.shape
    spot = [jax.random.randint(jax.random.fold_in(key, axis), (), 0, extent[axis]) for axis in range(len(extent))]
    array = array.at[tuple(spot)].set(low)
    longest = extent.index(max(extent))
    spot[longest] = (spot[longest] + 1) % extent[longest]
    return array.at[tuple(spot)].set(high)


def steps_of(stream_key, extent, shards, low, largest):
    level = 1.0
    for dim, blocks in shards:
        heights = jax.random.uniform(jax.random.fold_in(jax.random.fold_in(stream_key, 6), dim), (blocks,), jnp.float32, low / len(shards), largest / len(shards))
        level = level * jnp.repeat(jnp.exp(heights), extent[dim] // blocks).reshape((-1,) + (1,) * (len(extent) - 1 - dim))
    return level


def noise(own_key, dims, spread, limit, cuts=(), kind=jnp.bfloat16):
    factor_of = steps_of(own_key, dims, cuts, -0.22, 0.18) if cuts else 1.0
    entries = jax.random.normal(own_key, dims, jnp.float32) * spread * factor_of
    return jnp.minimum(jnp.maximum(entries, -limit), limit).astype(kind)


def setup_inputs(seed: int = 0) -> dict:
    seeds = jax.random.split(jax.random.key(seed), 11)
    return {
        "costate": noise(seeds[0], (ADOS, 2, NL, NL), 1.0, 6.0, ((0, 32),)),
        "hamiltonian": noise(seeds[1], (NL, NL), NL ** -0.5, 0.375),
        "couplers": noise(seeds[2], (OPS, NL, NL), NL ** -0.5, 0.375),
        "damping": jnp.clip(jnp.exp(jax.random.uniform(seeds[3], (MODES,), jnp.float32, math.log(0.05), math.log(0.5))), 0.05, 0.5),
        "coupling": noise(seeds[4], (2, MODES), 0.3, 0.9, (), jnp.float32),
        "levels": set_ends(jax.random.randint(seeds[5], (ADOS, MODES), 0, 4), jax.random.fold_in(seeds[5], 1), 0, 3).astype(jnp.int32),
        "neighbour_slot": set_ends(jax.random.randint(seeds[6], (ADOS, NEIGH), 0, SLOTS), jax.random.fold_in(seeds[6], 1), 0, SLOTS - 1).astype(jnp.int32),
        "neighbour_mode": set_ends(jax.random.randint(seeds[7], (ADOS, NEIGH), 0, MODES), jax.random.fold_in(seeds[7], 1), 0, MODES - 1).astype(jnp.int32),
        "neighbour_flag": set_ends(jax.random.randint(seeds[8], (ADOS, NEIGH), -1, 2), jax.random.fold_in(seeds[8], 1), -1, 1).astype(jnp.int32),
        "send_index": set_ends(jax.random.randint(seeds[9], (BLOCKS, SLOTS), 0, MB_DEV), jax.random.fold_in(seeds[9], 1), 0, MB_DEV - 1).astype(jnp.int32),
    }


def symmetric(weight):
    square = weight.astype(jnp.float32)
    return ((square + jnp.swapaxes(square, -1, -2)) * 0.5).astype(jnp.bfloat16)

def evaluate(state, operators, damping, coupling, levels, neighbour_slot, neighbour_mode, neighbour_flag, send_index):
    high = lax.Precision.HIGHEST
    opfloat = operators.astype(jnp.float32)

    def single(index):
        block = index // MB_DEV
        tier_here = block // N_MAT
        group = block % N_MAT
        slot = neighbour_slot[index]
        provider = slot // CAP * N_MAT + group
        position = slot % CAP
        source = (provider * MB_DEV + send_index[provider, tier_here * CAP + position]).astype(jnp.int32)
        gathered = state[source].astype(jnp.float32)
        own = state[index].astype(jnp.float32)
        mode = neighbour_mode[index]
        flag = neighbour_flag[index]
        live = (flag >= 0).astype(jnp.float32)
        weight = jnp.sqrt(1.0 + levels[index][mode].astype(jnp.float32)) * live
        coup_real = coupling[0][mode] * weight
        coup_imag = coupling[1][mode] * weight
        right_imag = jnp.where(flag == 1, coup_imag, -coup_imag)
        select = (mode[None, :] % 3 == jnp.arange(3)[:, None]).astype(jnp.float32)

        def combine(real_part, imag_part):
            creal = select * real_part[None, :]
            cimag = select * imag_part[None, :]
            sreal = jnp.einsum('qe,eij->qij', creal, gathered[:, 0], precision=high) - jnp.einsum('qe,eij->qij', cimag, gathered[:, 1], precision=high)
            simag = jnp.einsum('qe,eij->qij', creal, gathered[:, 1], precision=high) + jnp.einsum('qe,eij->qij', cimag, gathered[:, 0], precision=high)
            return jnp.stack([sreal, simag], 1).astype(jnp.bfloat16)
        left_in = combine(coup_real, coup_imag)
        right_in = combine(coup_real, right_imag)
        rotated = jnp.stack([-state[index][1], state[index][0]])[None]
        left_all = jnp.concatenate([rotated, left_in], 0).astype(jnp.float32)
        right_all = jnp.concatenate([rotated, right_in], 0).astype(jnp.float32)
        left = jnp.einsum('oij,opjk->pik', opfloat, left_all, precision=high)
        right = jnp.einsum('opij,ojk->pik', right_all, opfloat, precision=high)
        decay = jnp.sum(levels[index].astype(jnp.float32) * damping)
        rate = left - right - decay * own
        correlation = jnp.einsum('pij,epij->e', own, gathered, precision=high)
        onehot = (mode[:, None] == jnp.arange(MODES)[None, :]).astype(jnp.float32)
        grad = jnp.dot(correlation * weight / NL, onehot, precision=high)
        return (rate, grad)
    rates, grads = lax.map(single, jnp.arange(state.shape[0], dtype=jnp.int32))
    return (rates, lax.optimization_barrier(jnp.sum(grads, 0)))

def reference(costate, hamiltonian, couplers, damping, coupling, levels, neighbour_slot, neighbour_mode, neighbour_flag, send_index):
    operators = jnp.concatenate([symmetric(hamiltonian)[None], symmetric(couplers)], 0)
    first, grad_first = evaluate(costate, operators, damping, coupling, levels, neighbour_slot, neighbour_mode, neighbour_flag, send_index)
    middle = (costate.astype(jnp.float32) + 0.125 * first).astype(jnp.bfloat16)
    second, grad_second = evaluate(middle, operators, damping, coupling, levels, neighbour_slot, neighbour_mode, neighbour_flag, send_index)
    return (0.25 * second, grad_first + grad_second)
```

```python
import functools

import jax
import jax.numpy as jnp
from jax import lax
from jax.experimental import pallas as pl
from jax.experimental.pallas import tpu as pltpu
from jax.sharding import PartitionSpec as P

PIECES = 4
SUB = 8
LANES = 128
KINDS = 10
PAD = 16
F32 = jnp.float32
BF16 = jnp.bfloat16
MESH = pl.DeviceIdType.MESH
HIGH = lax.Precision.HIGHEST


def iota(shape, axis):
    return lax.broadcasted_iota(jnp.int32, shape, axis)


def exact(a, b, dims=(((1,), (0,)), ((), ()))):
    return lax.dot_general(a, b, dims, precision=HIGH, preferred_element_type=F32)


TURNED = (((1,), (1,)), ((), ()))


def dot(a, b):
    return jnp.dot(a, b, preferred_element_type=F32)


def column(row):
    n = row.shape[1]
    square = (n, n)
    return jnp.sum(jnp.where(iota(square, 0) == iota(square, 1), row, 0.0), 1, keepdims=True)


def when(cond, act):
    if cond is None:
        act()
    else:
        pl.when(cond)(act)


def kernel(
    tiers,
    mats,
    state_ref,
    ham_ref,
    coup_ref,
    damping_ref,
    strength_ref,
    levels_ref,
    slot_ref,
    mode_ref,
    flag_ref,
    index_ref,
    out_ref,
    grad_ref,
    acc,
    middle,
    left_in,
    right_in,
    left_ops,
    right_ops,
    mix_first,
    mix_second,
    slots_coef,
    slots_weight,
    mats_coef,
    mats_weight,
    place,
    decays,
    padded,
    own_index,
    all_index,
    chosen,
    tables,
    corr_first,
    corr_second,
    partial,
    by_tier,
    subtotal,
    by_mat,
    block_send,
    block_land,
    index_send,
    index_land,
    table_send,
    table_land,
    tier_send,
    tier_land,
    mat_send,
    mat_land,
    *gathered,
):
    count, _, width, _ = state_ref.shape
    modes = levels_ref.shape[1]
    near = slot_ref.shape[1]
    slots = index_ref.shape[1]
    cap = slots // tiers
    total = tiers * count
    piece = width // PIECES
    chunks = piece // SUB
    tall = count * SUB
    groups = (slots + count) // count
    last_group = groups - 1
    cols = 2
    while cols * cols * 2 < tiers:
        cols *= 2
    rows = tiers // cols
    detour = [k for k in range(PIECES) if k % 2 == 1] if cols == 2 else []

    me, mat = lax.axis_index("tier"), lax.axis_index("mat")
    z, y = me // cols, lax.rem(me, cols)
    tier_peers = [(lax.rem(me + d, tiers), mat) for d in range(1, tiers)]
    mat_peers = [(me, lax.rem(mat + d, mats)) for d in range(1, mats)]

    barrier = pltpu.get_barrier_semaphore()
    for device in tier_peers + mat_peers:
        pl.semaphore_signal(barrier, inc=1, device_id=device, device_id_type=MESH)

    def relayout(k):
        @pl.loop(0, chunks // 2)
        def _(step):
            at = pl.ds(pl.multiple_of(k * piece + step * 2 * SUB, 2 * SUB), 2 * SUB)
            for part in range(2):
                both = state_ref[:, part, at, :].astype(F32)
                for h in range(2):
                    eight = both[:, h * SUB : (h + 1) * SUB].reshape(tall, width)
                    gathered[k][me, part, step * 2 + h] = eight.astype(BF16)

    relayout(0)
    own_index[...] = jnp.full((SUB, LANES), -1, jnp.int32)
    own_index[0:1, 0:slots] = index_ref[...]
    pl.semaphore_wait(barrier, len(tier_peers) + len(mat_peers))

    below = (jnp.maximum(z - 1, 0) * cols + y, mat)
    above = (jnp.minimum(z + 1, rows - 1) * cols + y, mat)
    beside = [(z * cols + lax.rem(y + c, cols), mat) for c in range(1, cols)]
    ways = [below, above] + beside
    sides = range(2, 2 + len(beside))
    sent = []

    def copy(k, u, way):
        return pltpu.make_async_remote_copy(
            src_ref=gathered[k].at[u],
            dst_ref=gathered[k].at[u],
            send_sem=block_send.at[way, k, u],
            recv_sem=block_land.at[k, u],
            device_id=ways[way],
            device_id_type=MESH,
        )

    def go(k, u, way, cond=None):
        one = copy(k, u, way)
        sent.append((one, cond))
        when(cond, one.start)

    def got(k, u, cond=None):
        when(cond, copy(k, u, 2).wait_recv)

    def start_own(k):
        for way in sides:
            go(k, me, way)
        go(k, me, 0, z > 0)
        go(k, me, 1, z < rows - 1)

    def tier_at(row, col):
        return jnp.clip(row, 0, rows - 1) * cols + col

    def along(k, d):
        cond, u = z + d < rows, tier_at(z + d, y)
        got(k, u, cond)
        go(k, u, 0, cond & (z > 0))
        for way in sides:
            go(k, u, way, cond & (z + d != rows - 1) if k in detour else cond)
        cond, u = z - d >= 0, tier_at(z - d, y)
        got(k, u, cond)
        go(k, u, 1, cond & (z < rows - 1))
        for way in sides:
            go(k, u, way, cond & (z - d != 0) if k in detour else cond)

    def across(k):
        for c in range(1, cols):
            u = z * cols + lax.rem(y + c, cols)
            got(k, u)
            if k in detour:
                go(k, u, 0, z == rows - 1)
                go(k, u, 1, z == 0)

    def around(k):
        if k in detour:
            other = 1 - y
            cond, u = z < rows - 1, tier_at(rows - 1, other)
            got(k, u, cond)
            go(k, u, 0, cond & (z > 0))
            cond, u = z > 0, tier_at(0, other)
            got(k, u, cond)
            go(k, u, 1, cond & (z < rows - 1))

    def rest(k):
        for d in range(1, rows):
            for c in range(1, cols):
                col = lax.rem(y + c, cols)
                cond = z + d < rows
                if k in detour:
                    cond = cond & (z + d != rows - 1)
                got(k, tier_at(z + d, col), cond)
                cond = z - d >= 0
                if k in detour:
                    cond = cond & (z - d != 0)
                got(k, tier_at(z - d, col), cond)

    def events(k):
        def first():
            along(k, 1)
            across(k)
            if k + 2 < PIECES:
                start_own(k + 2)

        acts = [first]
        acts += [functools.partial(along, k, d) for d in range(2, rows)]
        acts.append(functools.partial(around, k))
        return acts

    start_own(0)
    index_copies = [
        pltpu.make_async_remote_copy(
            src_ref=own_index,
            dst_ref=all_index.at[me],
            send_sem=index_send.at[d],
            recv_sem=index_land.at[d],
            device_id=device,
            device_id_type=MESH,
        )
        for d, device in enumerate(tier_peers)
    ]
    for one in index_copies:
        one.start()
    all_index[me] = own_index[...]
    relayout(1)
    start_own(1)
    for k in range(2, PIECES):
        relayout(k)

    for i, ref in enumerate((slot_ref, mode_ref, flag_ref)):
        padded[i] = jnp.full((SUB, LANES), -1, jnp.int32)
        padded[i, 0:count, 0:near] = ref[...]
    shape = (PAD, LANES)
    kind = iota(shape, 0)
    lane = iota(shape, 1)
    mode_slot = iota(shape, 0)
    strong = [column(strength_ref[i : i + 1, :]) for i in range(2)]

    def tallest(col):
        return jnp.concatenate([col, jnp.zeros((PAD - col.shape[0], 1), F32)], 0)

    strong = [tallest(v) for v in strong]
    levels = levels_ref[...].astype(F32)
    fade = jnp.sum(levels * damping_ref[...], 1, keepdims=True)
    for n in range(count):
        slot, mode, flag = (padded[i, n : n + 1, :] for i in range(3))
        hot = (mode_slot == mode).astype(F32)
        live = (flag >= 0).astype(F32)
        level = tallest(column(levels[n : n + 1, :]))
        weight = jnp.sqrt(1.0 + jnp.sum(hot * level, 0, keepdims=True)) * live
        real = jnp.sum(hot * strong[0], 0, keepdims=True) * weight
        imag = jnp.sum(hot * strong[1], 0, keepdims=True) * weight
        other = jnp.where(flag == 1, imag, -imag)
        third = jnp.zeros_like(mode)
        for k in range(modes):
            third = jnp.where(mode == k, k % 3, third)
        values = jnp.where(kind < 4, real, jnp.where(kind < 7, imag, other))
        which = jnp.where(kind < 4, kind - 1, jnp.where(kind < 7, kind - 4, kind - 7))
        values = jnp.where((which == third) & (kind >= 1) & (kind < KINDS), values, 0.0)
        slot_hot = (iota((LANES, LANES), 0) == slot).astype(F32)
        at = slice(n * PAD, (n + 1) * PAD)
        slots_coef[at, :] = exact(values, slot_hot, TURNED)
        slots_weight[at, :] = exact(hot * weight, slot_hot, TURNED)

    for one in index_copies:
        one.wait()
    place[...] = jnp.full((LANES, LANES), -1, jnp.int32)
    row = iota((1, LANES), 1)
    for u in range(tiers):
        for s in range(cap):
            index = all_index[u, 0:1, :]
            index = jnp.sum(jnp.where(row == me * cap + s, index, 0), 1, keepdims=True)
            place[u * cap + s : u * cap + s + 1, :] = jnp.broadcast_to(index + u * count, (1, LANES))
    to_mat = (place[...] == iota((LANES, LANES), 1)).astype(F32)
    full = (count * PAD, LANES)
    spread = exact(slots_coef[...], to_mat)
    for n in range(count):
        own = jnp.where((kind == 0) & (lane == me * count + n), 1.0, 0.0)
        drop = jnp.where(kind == KINDS, fade[n : n + 1, :], 0.0)
        mats_coef[n * PAD : (n + 1) * PAD, :] = spread[n * PAD : (n + 1) * PAD] + own + drop
    mats_weight[...] = exact(slots_weight[...], to_mat)

    for t in range(tiers):
        for s in range(cap):
            index = own_index[0:1, t * cap + s : t * cap + s + 1]
            rows_of = jnp.zeros(shape, F32)
            for n in range(count):
                rows_of = jnp.where(index == n, mats_coef[n * PAD : (n + 1) * PAD, :], rows_of)
            chosen[t, s * PAD : (s + 1) * PAD, :] = rows_of
    table_copies = [
        pltpu.make_async_remote_copy(
            src_ref=chosen.at[device[0]],
            dst_ref=tables.at[me],
            send_sem=table_send.at[d],
            recv_sem=table_land.at[d],
            device_id=device,
            device_id_type=MESH,
        )
        for d, device in enumerate(tier_peers)
    ]
    for one in table_copies:
        one.start()
    tables[me] = chosen[me]

    for q in range(4):
        raw = (ham_ref[...] if q == 0 else coup_ref[q - 1]).astype(F32)
        right_ops[q * width : (q + 1) * width, :] = ((raw + raw.T) * 0.5).astype(BF16)
    for k in range(PIECES):
        stack = jnp.concatenate(
            [right_ops[q * width + k * piece : q * width + (k + 1) * piece, :] for q in range(4)], 0
        )
        left_ops[k] = stack.astype(F32).T.astype(BF16)

    def blow(ref, base, table, kinds, first, across_):
        deep = iota((kinds * SUB, PAD), 0)
        down = ((deep >= (iota((kinds * SUB, PAD), 1) - first) * SUB) & (deep < (iota((kinds * SUB, PAD), 1) - first + 1) * SUB)).astype(BF16)
        big = dot(down, table.astype(BF16)).astype(BF16)
        big = dot(big, across_)
        keep = (iota(big.shape, 0) & (SUB - 1)) == (iota(big.shape, 1) & (SUB - 1))
        ref[base, :] = jnp.where(keep, big, 0.0).astype(BF16)

    def widening(count_):
        wide = (LANES, count_ * SUB)
        deep = iota(wide, 0) * SUB
        return ((iota(wide, 1) >= deep) & (iota(wide, 1) < deep + SUB)).astype(BF16)

    by_slot = widening(slots)
    high = KINDS - 1
    for n in range(count):
        blow(
            mix_second,
            slice(n * high * SUB, (n + 1) * high * SUB),
            slots_coef[n * PAD : (n + 1) * PAD, :],
            high,
            1,
            by_slot,
        )
    corr_first[...] = jnp.zeros(corr_first.shape, F32)
    corr_second[...] = jnp.zeros(corr_second.shape, F32)

    for act in events(0):
        act()

    for one in table_copies:
        one.wait()
    by_matrix = widening(total)
    deep = KINDS * SUB

    @pl.loop(0, tiers)
    def _(u):
        for s in range(cap):
            table = tables[u, s * PAD : (s + 1) * PAD, :]
            base = pl.ds(pl.multiple_of((u * cap + s) * deep, 2 * SUB), deep)
            blow(mix_first, base, table, KINDS, 0, by_matrix)
            decays[u * cap + s] = jnp.broadcast_to(table[KINDS : KINDS + 1, 0:1], (1, width))

    for n in range(count):
        table = mats_coef[n * PAD : (n + 1) * PAD, :]
        blow(mix_first, pl.ds((slots + n) * deep, deep), table, KINDS, 0, by_matrix)
        decays[slots + n] = jnp.broadcast_to(table[KINDS : KINDS + 1, 0:1], (1, width))

    def mix(coef, kinds, take, own_take, k):
        @pl.loop(0, chunks // 2)
        def _(step):
            parts = []
            for h in range(2):
                c = step * 2 + h
                parts.append([dot(coef, take(part, c)).reshape(count, kinds, SUB, width) for part in range(2)])
            at = pl.ds(pl.multiple_of(step * 2 * SUB, 2 * SUB), 2 * SUB)

            def both(make):
                return jnp.concatenate([make(h) for h in range(2)], -2).astype(BF16)

            if own_take is None:
                x = lambda h, part: parts[h][part][:, 0]
            else:
                x = lambda h, part: own_take(part, step * 2 + h)
            turned = (both(lambda h: -x(h, 1)), both(lambda h: x(h, 0)))
            a = kinds - 9
            b, c = a + 3, a + 6
            lefts = (
                both(lambda h: parts[h][0][:, a:b] - parts[h][1][:, b:c]),
                both(lambda h: parts[h][1][:, a:b] + parts[h][0][:, b:c]),
            )
            rights = (
                both(lambda h: parts[h][0][:, a:b] - parts[h][1][:, c:]),
                both(lambda h: parts[h][1][:, a:b] + parts[h][0][:, c:]),
            )
            for part in range(2):
                left_in[:, part, 0, at, :] = turned[part]
                left_in[:, part, 1:, at, :] = lefts[part]
                right_in[:, part, at, 0:width] = turned[part]
                for q in range(3):
                    right_in[:, part, at, (q + 1) * width : (q + 2) * width] = rights[part][:, q]

    def apply(k, base, scale, finish):
        at = slice(k * piece, (k + 1) * piece)

        def products(n, part):
            return dot(left_ops[k], left_in[n, part].reshape(4 * piece, width))

        def local():
            back = dot(right_in[...].reshape(count * 2 * piece, 4 * width), right_ops[...])
            back = back.reshape(count, 2, piece, width)
            for n in range(count):
                keep = scale - decays[base + n]
                for part in range(2):
                    x = left_in[n, 1 - part, 0].astype(F32)
                    x = x if part == 0 else -x
                    acc[base + n, part, at, :] += keep * x - back[n, part]

        if k > 0:
            local()
        if finish is None:
            for n in range(count):
                for part in range(2):
                    if k == 0:
                        acc[base + n, part] = products(n, part)
                    else:
                        acc[base + n, part] += products(n, part)
        else:
            finish(lambda n, part: acc[base + n, part] + products(n, part))
        if k == 0:
            local()

    def first_section(k, start, stop):
        def take(part, c):
            return gathered[k][:, part, c].reshape(total * SUB, width)

        @pl.loop(start, stop)
        def _(g):
            tall_rows = count * deep
            coef = mix_first[pl.ds(pl.multiple_of(g * tall_rows, 2 * SUB), tall_rows), :]
            mix(coef, KINDS, take, None, k)

            def finish(value):
                for part in range(2):
                    for n in range(0, count, 2):
                        pair = [
                            (0.125 * value(n + i, part)).reshape(width // SUB, SUB, width)
                            for i in range(2)
                        ]
                        at = pl.ds(pl.multiple_of(g * tall + n * SUB, 2 * SUB), 2 * SUB)
                        middle[part, :, at, :] = jnp.concatenate(pair, 1).astype(BF16)

            apply(k, g * count, 1 / 0.125, finish if k == PIECES - 1 else None)

    def correlate_first(k):
        @pl.loop(0, chunks)
        def _(c):
            for part in range(2):
                corr_first[...] += lax.dot_general(
                    gathered[k][:, part, c].reshape(total * SUB, width),
                    gathered[k][me, part, c],
                    TURNED,
                    preferred_element_type=F32,
                )

    for k in range(PIECES):
        rest(k)
        later = events(k + 1) if k + 1 < PIECES else []
        if later:
            later.pop(0)()
        correlate_first(k)
        cut = [0] + [(i + 1) * groups // 2 for i in range(2)]
        for i in range(2):
            first_section(k, cut[i], cut[i + 1])
            if later:
                later.pop(0)()
        for act in later:
            act()

    own_at = slice(slots * SUB, slots * SUB + tall)

    @pl.loop(0, width // SUB)
    def _(c):
        for part in range(2):
            corr_second[...] += lax.dot_general(
                middle[part, c, 0 : slots * SUB, :],
                middle[part, c, own_at, :],
                TURNED,
                preferred_element_type=F32,
            )

    def gradient(corr, weights, how_many):
        shape_ = corr.shape
        keep = (iota(shape_, 0) & (SUB - 1)) == (iota(shape_, 1) & (SUB - 1))
        kept = jnp.where(keep, corr[...], 0.0)
        gather = (SUB, tall)
        begin = iota(gather, 0) * SUB
        pick = ((iota(gather, 1) >= begin) & (iota(gather, 1) < begin + SUB)).astype(F32)
        wide = exact(pick, kept, TURNED)
        narrow = (how_many * SUB, LANES)
        begin = iota(narrow, 1) * SUB
        pick = ((iota(narrow, 0) >= begin) & (iota(narrow, 0) < begin + SUB)).astype(F32)
        pairs = exact(wide, pick)
        sums = jnp.zeros(shape, F32)
        for n in range(count):
            sums += weights[n * PAD : (n + 1) * PAD, :] * pairs[n : n + 1, :]
        return sums

    sums = gradient(corr_first, mats_weight, total) + gradient(corr_second, slots_weight, slots)
    sums = jnp.concatenate([sums, jnp.zeros((LANES - PAD, LANES), F32)], 0)
    partial[...] = exact(jnp.full((SUB, LANES), 1.0 / width, F32), sums, TURNED)
    tier_copies = [
        pltpu.make_async_remote_copy(
            src_ref=partial,
            dst_ref=by_tier.at[me],
            send_sem=tier_send.at[d],
            recv_sem=tier_land.at[d],
            device_id=device,
            device_id_type=MESH,
        )
        for d, device in enumerate(tier_peers)
    ]
    for one in tier_copies:
        one.start()
    by_tier[me] = partial[...]

    coef = mix_second[...]
    own_base = last_group * count
    mat_copies = []
    for k in range(PIECES):

        def take(part, c):
            return middle[part, k * chunks + c, 0 : slots * SUB, :]

        def own_take(part, c):
            return middle[part, k * chunks + c, own_at, :].astype(F32).reshape(count, SUB, width)

        mix(coef, KINDS - 1, take, own_take, k)

        def finish(value):
            for n in range(count):
                for part in range(2):
                    out_ref[n, part] = 0.25 * value(n, part)

        apply(k, own_base, 0.0, finish if k == PIECES - 1 else None)
        if k == 0:
            for one in tier_copies:
                one.wait()
            subtotal[...] = jnp.sum(by_tier[...], 0)
            by_mat[mat] = subtotal[...]
            mat_copies = [
                pltpu.make_async_remote_copy(
                    src_ref=subtotal,
                    dst_ref=by_mat.at[mat],
                    send_sem=mat_send.at[d],
                    recv_sem=mat_land.at[d],
                    device_id=device,
                    device_id_type=MESH,
                )
                for d, device in enumerate(mat_peers)
            ]
            for one in mat_copies:
                one.start()

    for one in mat_copies:
        one.wait()
    grad_ref[...] = jnp.sum(by_mat[...], 0)[0:1, 0:modes]
    for one, cond in sent:
        when(cond, one.wait_send)


def per_device(
    tiers,
    mats,
    costate,
    hamiltonian,
    couplers,
    damping,
    coupling,
    levels,
    neighbour_slot,
    neighbour_mode,
    neighbour_flag,
    send_index,
):
    count, _, width, _ = costate.shape
    modes = levels.shape[1]
    slots = send_index.shape[1]
    cap = slots // tiers
    total = tiers * count
    targets = slots + count
    piece = width // PIECES
    tall = count * SUB
    cols = 2
    while cols * cols * 2 < tiers:
        cols *= 2
    vmem = pl.BlockSpec(memory_space=pltpu.VMEM)
    dma = pltpu.SemaphoreType.DMA

    def small(*lead):
        return pltpu.VMEM(lead + (SUB, LANES), F32)

    increment, grads = pl.pallas_call(
        functools.partial(kernel, tiers, mats),
        out_shape=(
            jax.ShapeDtypeStruct(costate.shape, F32),
            jax.ShapeDtypeStruct((1, modes), F32),
        ),
        in_specs=[vmem] * 10,
        out_specs=(vmem, vmem),
        scratch_shapes=[
            pltpu.VMEM((targets, 2, width, width), F32),
            pltpu.VMEM((2, width // SUB, targets * SUB, width), BF16),
            pltpu.VMEM((count, 2, 4, piece, width), BF16),
            pltpu.VMEM((count, 2, piece, 4 * width), BF16),
            pltpu.VMEM((PIECES, width, 4 * piece), BF16),
            pltpu.VMEM((4 * width, width), BF16),
            pltpu.VMEM((targets * KINDS * SUB, total * SUB), BF16),
            pltpu.VMEM((count * (KINDS - 1) * SUB, slots * SUB), BF16),
            pltpu.VMEM((count * PAD, LANES), F32),
            pltpu.VMEM((count * PAD, LANES), F32),
            pltpu.VMEM((count * PAD, LANES), F32),
            pltpu.VMEM((count * PAD, LANES), F32),
            pltpu.VMEM((LANES, LANES), jnp.int32),
            pltpu.VMEM((targets, 1, width), F32),
            pltpu.VMEM((3, SUB, LANES), jnp.int32),
            pltpu.VMEM((SUB, LANES), jnp.int32),
            pltpu.VMEM((tiers, SUB, LANES), jnp.int32),
            pltpu.VMEM((tiers, cap * PAD, LANES), F32),
            pltpu.VMEM((tiers, cap * PAD, LANES), F32),
            pltpu.VMEM((total * SUB, tall), F32),
            pltpu.VMEM((slots * SUB, tall), F32),
            small(),
            small(tiers),
            small(),
            small(mats),
            dma((1 + cols, PIECES, tiers)),
            dma((PIECES, tiers)),
        ]
        + [dma((tiers - 1,))] * 6
        + [dma((mats - 1,))] * 2
        + [pltpu.VMEM((tiers, 2, piece // SUB, tall, width), BF16)] * PIECES,
        compiler_params=pltpu.CompilerParams(
            vmem_limit_bytes=60 << 20, collective_id=0, has_side_effects=True
        ),
        name="midpoint",
    )(
        costate,
        hamiltonian,
        couplers,
        damping[None, :],
        coupling,
        levels,
        neighbour_slot,
        neighbour_mode,
        neighbour_flag,
        send_index,
    )
    return increment, grads[0]


def solution(mesh):
    blocks = P(("tier", "mat"), None)
    return jax.shard_map(
        functools.partial(per_device, mesh.shape["tier"], mesh.shape["mat"]),
        mesh=mesh,
        in_specs=(P(("tier", "mat"), None, None, None), P(), P(), P(), P()) + (blocks,) * 5,
        out_specs=(P(("tier", "mat"), None, None, None), P()),
        check_vma=False,
    )
```

```python
import functools

import jax
import jax.numpy as jnp
from jax import lax
from jax.experimental import pallas as pl
from jax.experimental.pallas import tpu as pltpu
from jax.sharding import PartitionSpec as P

SHARES = (4, 4, 4, 2, 2)
DETOUR = (1, 2)
ROUNDS = ((0, 1), (2,3), (4,))
PIECES = len(SHARES)
SUB = 8
LANES = 128
KINDS = 10
PAD = 16
F32 = jnp.float32
BF16 = jnp.bfloat16
MESH = pl.DeviceIdType.MESH
HIGH = lax.Precision.HIGHEST


def iota(shape, axis):
    return lax.broadcasted_iota(jnp.int32, shape, axis)


def exact(a, b, dims=(((1,), (0,)), ((), ()))):
    return lax.dot_general(a, b, dims, precision=HIGH, preferred_element_type=F32)


TURNED = (((1,), (1,)), ((), ()))


def dot(a, b):
    return jnp.dot(a, b, preferred_element_type=F32)


def column(row):
    n = row.shape[1]
    square = (n, n)
    return jnp.sum(jnp.where(iota(square, 0) == iota(square, 1), row, 0.0), 1, keepdims=True)


def when(cond, act):
    if cond is None:
        act()
    else:
        pl.when(cond)(act)


def kernel(
    tiers,
    mats,
    state_ref,
    ham_ref,
    coup_ref,
    damping_ref,
    strength_ref,
    levels_ref,
    slot_ref,
    mode_ref,
    flag_ref,
    index_ref,
    out_ref,
    grad_ref,
    acc,
    middle,
    left_in,
    right_in,
    right_ops,
    mix_first,
    mix_second,
    slots_coef,
    slots_weight,
    mats_coef,
    mats_turned,
    slots_turned,
    place,
    decays,
    padded,
    own_index,
    all_index,
    chosen,
    tables,
    corr_first,
    corr_second,
    partial,
    by_tier,
    subtotal,
    by_mat,
    block_send,
    block_land,
    index_send,
    index_land,
    table_send,
    table_land,
    tier_send,
    tier_land,
    mat_send,
    mat_land,
    *by_piece,
):
    gathered, left_ops = by_piece[:PIECES], by_piece[PIECES:]
    count, _, width, _ = state_ref.shape
    modes = levels_ref.shape[1]
    near = slot_ref.shape[1]
    slots = index_ref.shape[1]
    cap = slots // tiers
    total = tiers * count
    sizes = [share * width // sum(SHARES) for share in SHARES]
    starts = [sum(sizes[:k]) for k in range(PIECES)]
    tall = count * SUB
    groups = (slots + count) // count
    last_group = groups - 1
    cols = 2
    while cols * cols * 2 < tiers:
        cols *= 2
    rows = tiers // cols
    detour = DETOUR if cols == 2 else ()
    batch = max(b for b in range(1, 6) if groups % b == 0) * count

    me, mat = lax.axis_index("tier"), lax.axis_index("mat")
    z, y = me // cols, lax.rem(me, cols)
    tier_peers = [(lax.rem(me + d, tiers), mat) for d in range(1, tiers)]
    mat_peers = [(me, lax.rem(mat + d, mats)) for d in range(1, mats)]

    barrier = pltpu.get_barrier_semaphore()
    for device in tier_peers + mat_peers:
        pl.semaphore_signal(barrier, inc=1, device_id=device, device_id_type=MESH)

    def relayout(k):
        @pl.loop(0, sizes[k] // (2 * SUB))
        def _(step):
            at = pl.ds(pl.multiple_of(starts[k] + step * 2 * SUB, 2 * SUB), 2 * SUB)
            for part in range(2):
                both = state_ref[:, part, at, :].astype(F32)
                for h in range(2):
                    eight = both[:, h * SUB : (h + 1) * SUB].reshape(tall, width)
                    gathered[k][me, part, step * 2 + h] = eight.astype(BF16)

    relayout(0)
    own_index[...] = jnp.full((SUB, LANES), -1, jnp.int32)
    own_index[0:1, 0:slots] = index_ref[...]
    pl.semaphore_wait(barrier, len(tier_peers) + len(mat_peers))

    below = (jnp.maximum(z - 1, 0) * cols + y, mat)
    above = (jnp.minimum(z + 1, rows - 1) * cols + y, mat)
    beside = [(z * cols + lax.rem(y + c, cols), mat) for c in range(1, cols)]
    ways = [below, above] + beside
    sides = range(2, 2 + len(beside))
    sent = []

    def copy(k, u, way):
        return pltpu.make_async_remote_copy(
            src_ref=gathered[k].at[u],
            dst_ref=gathered[k].at[u],
            send_sem=block_send.at[way, k, u],
            recv_sem=block_land.at[k, u],
            device_id=ways[way],
            device_id_type=MESH,
        )

    def go(k, u, way, cond=None):
        one = copy(k, u, way)
        sent.append((one, cond))
        when(cond, one.start)

    def got(k, u, cond=None):
        when(cond, copy(k, u, 2).wait_recv)

    def start_own(k):
        for way in sides:
            go(k, me, way)
        go(k, me, 0, z > 0)
        go(k, me, 1, z < rows - 1)

    def tier_at(row, col):
        return jnp.clip(row, 0, rows - 1) * cols + col

    def along(k, d):
        cond, u = z + d < rows, tier_at(z + d, y)
        if k in detour and d == rows - 1:
            return
        got(k, u, cond)
        go(k, u, 0, cond & (z > 0))
        for way in sides:
            go(k, u, way, cond & (z + d != rows - 1) if k in detour else cond)
        cond, u = z - d >= 0, tier_at(z - d, y)
        got(k, u, cond)
        go(k, u, 1, cond & (z < rows - 1))
        for way in sides:
            go(k, u, way, cond & (z - d != 0) if k in detour else cond)

    def across(k):
        for c in range(1, cols):
            u = z * cols + lax.rem(y + c, cols)
            got(k, u)
            if k in detour:
                go(k, u, 0, z == rows - 1)
                go(k, u, 1, z == 0)

    def around(k):
        if k in detour:
            inner = (z < rows - 1) & (z > 0)
            for row, way in ((rows - 1, 0), (0, 1)):
                got(k, tier_at(row, 1 - y), inner)
                go(k, tier_at(row, 1 - y), way, inner)

    def rest(k):
        if k in detour:
            got(k, tier_at(rows - 1, 1 - y), z == 0)
            got(k, tier_at(0, 1 - y), z == rows - 1)
            got(k, tier_at(rows - 1, y), z == 0)
            got(k, tier_at(0, y), z == rows - 1)
        for d in range(1, rows):
            for c in range(1, cols):
                col = lax.rem(y + c, cols)
                cond = z + d < rows
                if k in detour:
                    cond = cond & (z + d != rows - 1)
                got(k, tier_at(z + d, col), cond)
                cond = z - d >= 0
                if k in detour:
                    cond = cond & (z - d != 0)
                got(k, tier_at(z - d, col), cond)

    def events(number):
        if number >= len(ROUNDS):
            return []
        pieces = ROUNDS[number]

        def first():
            for k in pieces:
                along(k, 1)
                across(k)
            if number + 1 < len(ROUNDS):
                for k in ROUNDS[number + 1]:
                    start_own(k)

        def further(d):
            for k in pieces:
                along(k, d)

        def last():
            for k in pieces:
                around(k)

        return [first] + [functools.partial(further, d) for d in range(2, rows)] + [last]

    index_copies = [
        pltpu.make_async_remote_copy(
            src_ref=own_index,
            dst_ref=all_index.at[me],
            send_sem=index_send.at[d],
            recv_sem=index_land.at[d],
            device_id=device,
            device_id_type=MESH,
        )
        for d, device in enumerate(tier_peers)
    ]
    for one in index_copies:
        one.start()
    start_own(0)
    all_index[me] = own_index[...]
    relayout(1)
    start_own(1)
    for k in range(2, PIECES):
        relayout(k)

    every = [events(number) for number in range(len(ROUNDS))]

    def step_on(*order):
        for k, i in order:
            if k < len(every) and i < len(every[k]) and every[k][i] is not None:
                every[k][i]()
                every[k][i] = None

    step_on((0, 0),)

    for i, ref in enumerate((slot_ref, mode_ref, flag_ref)):
        padded[i] = jnp.full((SUB, LANES), -1, jnp.int32)
        padded[i, 0:count, 0:near] = ref[...]
    shape = (PAD, LANES)
    kind = iota(shape, 0)
    lane = iota(shape, 1)
    mode_slot = iota(shape, 0)
    strong = [column(strength_ref[i : i + 1, :]) for i in range(2)]

    def tallest(col):
        return jnp.concatenate([col, jnp.zeros((PAD - col.shape[0], 1), F32)], 0)

    strong = [tallest(v) for v in strong]
    levels = levels_ref[...].astype(F32)
    fade = jnp.sum(levels * damping_ref[...], 1, keepdims=True)
    for n in range(count):
        slot, mode, flag = (padded[i, n : n + 1, :] for i in range(3))
        hot = (mode_slot == mode).astype(F32)
        live = (flag >= 0).astype(F32)
        level = tallest(column(levels[n : n + 1, :]))
        weight = jnp.sqrt(1.0 + jnp.sum(hot * level, 0, keepdims=True)) * live
        real = jnp.sum(hot * strong[0], 0, keepdims=True) * weight
        imag = jnp.sum(hot * strong[1], 0, keepdims=True) * weight
        other = jnp.where(flag == 1, imag, -imag)
        third = jnp.zeros_like(mode)
        for k in range(modes):
            third = jnp.where(mode == k, k % 3, third)
        values = jnp.where(kind < 4, real, jnp.where(kind < 7, imag, other))
        which = jnp.where(kind < 4, kind - 1, jnp.where(kind < 7, kind - 4, kind - 7))
        values = jnp.where((which == third) & (kind >= 1) & (kind < KINDS), values, 0.0)
        slot_hot = (iota((LANES, LANES), 0) == slot).astype(F32)
        at = slice(n * PAD, (n + 1) * PAD)
        slots_coef[at, :] = exact(values, slot_hot, TURNED)
        slots_weight[at, :] = exact(hot * weight, slot_hot, TURNED)

    step_on((0, 1))
    for one in index_copies:
        one.wait()
    place[...] = jnp.full((LANES, LANES), -1, jnp.int32)
    row = iota((1, LANES), 1)
    for u in range(tiers):
        for s in range(cap):
            index = all_index[u, 0:1, :]
            index = jnp.sum(jnp.where(row == me * cap + s, index, 0), 1, keepdims=True)
            place[u * cap + s : u * cap + s + 1, :] = jnp.broadcast_to(index + u * count, (1, LANES))
    to_mat = (place[...] == iota((LANES, LANES), 1)).astype(F32)
    spread = exact(slots_coef[...], to_mat)
    for n in range(count):
        own = jnp.where((kind == 0) & (lane == me * count + n), 1.0, 0.0)
        drop = jnp.where(kind == KINDS, fade[n : n + 1, :], 0.0)
        mats_coef[n * PAD : (n + 1) * PAD, :] = spread[n * PAD : (n + 1) * PAD] + own + drop
    def turned(table):
        return jnp.concatenate([table, jnp.zeros((LANES - count * PAD, LANES), F32)], 0).T

    mats_turned[...] = turned(exact(slots_weight[...], to_mat))
    slots_turned[...] = turned(slots_weight[...])

    for t in range(tiers):
        for s in range(cap):
            index = own_index[0:1, t * cap + s : t * cap + s + 1]
            rows_of = jnp.zeros(shape, F32)
            for n in range(count):
                rows_of = jnp.where(index == n, mats_coef[n * PAD : (n + 1) * PAD, :], rows_of)
            chosen[t, s * PAD : (s + 1) * PAD, :] = rows_of
    table_copies = [
        pltpu.make_async_remote_copy(
            src_ref=chosen.at[device[0]],
            dst_ref=tables.at[me],
            send_sem=table_send.at[d],
            recv_sem=table_land.at[d],
            device_id=device,
            device_id_type=MESH,
        )
        for d, device in enumerate(tier_peers)
    ]
    for one in table_copies:
        one.start()
    tables[me] = chosen[me]
    step_on((0, 2))

    def make_operators():
        for q in range(4):
            raw = (ham_ref[...] if q == 0 else coup_ref[q - 1]).astype(F32)
            op = ((raw + raw.T) * 0.5).astype(BF16)
            right_ops[q * width : (q + 1) * width, :] = op
            acc[q, 0] = op.astype(F32)
        for k in range(PIECES):
            stack = [
                acc[q, 0, r : r + SUB, :]
                for r in range(starts[k], starts[k] + sizes[k], SUB)
                for q in range(4)
            ]
            left_ops[k][...] = jnp.concatenate(stack, 0).T.astype(BF16)

    def blow(ref, base, table, kinds, first, across_):
        deep = iota((kinds * SUB, PAD), 0)
        down = ((deep >= (iota((kinds * SUB, PAD), 1) - first) * SUB) & (deep < (iota((kinds * SUB, PAD), 1) - first + 1) * SUB)).astype(BF16)
        big = dot(down, table.astype(BF16)).astype(BF16)
        big = dot(big, across_)
        keep = (iota(big.shape, 0) & (SUB - 1)) == (iota(big.shape, 1) & (SUB - 1))
        ref[base, :] = jnp.where(keep, big, 0.0).astype(BF16)

    def widening(count_):
        wide = (LANES, count_ * SUB)
        deep = iota(wide, 0) * SUB
        return ((iota(wide, 1) >= deep) & (iota(wide, 1) < deep + SUB)).astype(BF16)

    by_slot = widening(slots)
    high = KINDS - 1
    for n in range(count):
        blow(
            mix_second,
            slice(n * high * SUB, (n + 1) * high * SUB),
            slots_coef[n * PAD : (n + 1) * PAD, :],
            high,
            1,
            by_slot,
        )
    corr_first[...] = jnp.zeros(corr_first.shape, F32)
    corr_second[...] = jnp.zeros(corr_second.shape, F32)

    step_on((0, 3))
    make_operators()
    for one in table_copies:
        one.wait()
    by_matrix = widening(total)
    deep = KINDS * SUB

    @pl.loop(0, tiers)
    def _(u):
        for s in range(cap):
            table = tables[u, s * PAD : (s + 1) * PAD, :]
            base = pl.ds(pl.multiple_of((u * cap + s) * deep, 2 * SUB), deep)
            blow(mix_first, base, table, KINDS, 0, by_matrix)
            decays[u * cap + s] = jnp.broadcast_to(table[KINDS : KINDS + 1, 0:1], (1, width))

    step_on((1, 0))
    for n in range(count):
        table = mats_coef[n * PAD : (n + 1) * PAD, :]
        blow(mix_first, pl.ds((slots + n) * deep, deep), table, KINDS, 0, by_matrix)
        decays[slots + n] = jnp.broadcast_to(table[KINDS : KINDS + 1, 0:1], (1, width))

    def mix(coef, kinds, take, own_take, k, many):
        @pl.loop(0, sizes[k] // SUB)
        def _(c):
            real, imag = (
                dot(coef, take(part, c)).reshape(many, kinds, SUB, width) for part in range(2)
            )
            a = kinds - 9
            lefts_at = pl.ds(pl.multiple_of(c * 4 * SUB, 4 * SUB), 4 * SUB)
            for t in range(many):
                if own_take is None:
                    x = real[t, 0], imag[t, 0]
                else:
                    x = own_take(0, c)[t], own_take(1, c)[t]
                p, r = real[t, a:], imag[t, a:]
                lefts = [[-x[1]], [x[0]]]
                rights = [[-x[1], x[0]]]
                for q in range(3):
                    lefts[0].append(p[q] - r[3 + q])
                    lefts[1].append(r[q] + p[3 + q])
                    rights.append([p[q] - r[6 + q], r[q] + p[6 + q]])
                for part in range(2):
                    left_in[t, part, lefts_at, :] = jnp.concatenate(lefts[part], 0).astype(BF16)
                for q in range(4):
                    at = slice(q * width, (q + 1) * width)
                    right_in[t, c, :, at] = jnp.concatenate(rights[q], 0).astype(BF16)

    def apply(k, slot0, base, scale, finish):
        at = slice(starts[k], starts[k] + sizes[k])
        chunks = sizes[k] // SUB

        def products(n, part):
            return dot(left_ops[k][...], left_in[slot0 + n, part, 0 : 4 * sizes[k], :])

        def local():
            rows_in = right_in[pl.ds(slot0, count), 0:chunks]
            back = dot(rows_in.reshape(count * chunks * 2 * SUB, 4 * width), right_ops[...])
            back = back.reshape(count, chunks, 2, SUB, width)
            for n in range(count):
                keep = scale - decays[base + n]
                for part in range(2):
                    x = left_in[slot0 + n, 1 - part, 0 : 4 * sizes[k], :].astype(F32)
                    x = x.reshape(chunks, 4, SUB, width)[:, 0].reshape(sizes[k], width)
                    x = x if part == 0 else -x
                    acc[base + n, part, at, :] += keep * x - back[n, :, part].reshape(sizes[k], width)

        if k > 0:
            local()
        if finish is None:
            for n in range(count):
                for part in range(2):
                    if k == 0:
                        acc[base + n, part] = products(n, part)
                    else:
                        acc[base + n, part] += products(n, part)
        else:
            finish(lambda n, part: acc[base + n, part] + products(n, part))
        if k == 0:
            local()

    def first_mix(k, b):
        def take(part, c):
            return gathered[k][:, part, c].reshape(total * SUB, width)

        mix(mix_first[b * batch * deep : (b + 1) * batch * deep, :], KINDS, take, None, k, batch)

    def first_apply(k, b):
        @pl.loop(0, batch // count)
        def _(i):
            g = b * (batch // count) + i

            def finish(value):
                for part in range(2):
                    for n in range(0, count, 2):
                        pair = [
                            (0.125 * value(n + j, part)).reshape(width // SUB, SUB, width)
                            for j in range(2)
                        ]
                        at = pl.ds(pl.multiple_of(g * tall + n * SUB, 2 * SUB), 2 * SUB)
                        middle[part, :, at, :] = jnp.concatenate(pair, 1).astype(BF16)

            apply(k, i * count, g * count, 1 / 0.125, finish if k == PIECES - 1 else None)

    def correlate(target, rows_of, own_of):
        target[...] += lax.dot_general(
            jnp.concatenate(rows_of, 1),
            jnp.concatenate(own_of, 1),
            TURNED,
            preferred_element_type=F32,
        )

    def correlate_first(k):
        @pl.loop(0, sizes[k] // (2 * SUB))
        def _(step):
            spots = [(part, step * 2 + h) for part in range(2) for h in range(2)]
            correlate(
                corr_first,
                [gathered[k][:, part, c].reshape(total * SUB, width) for part, c in spots],
                [gathered[k][me, part, c] for part, c in spots],
            )

    for number, pieces in enumerate(ROUNDS):
        step_on(*((number, i) for i in range(rows + 1)), (number + 1, 0))
        todo = [(number + 1, i) for i in range(1, rows + 1)]
        for k in pieces:
            rest(k)
        for k in pieces:
            correlate_first(k)
            for b in range(groups * count // batch):
                first_mix(k, b)
                step_on(*todo[:1])
                first_apply(k, b)
                step_on(*todo[1:2])
                todo = todo[2:]
        step_on(*todo)

    own_at = slice(slots * SUB, slots * SUB + tall)

    @pl.loop(0, width // (2 * SUB))
    def _(step):
        spots = [(part, step * 2 + h) for part in range(2) for h in range(2)]
        correlate(
            corr_second,
            [middle[part, c, 0 : slots * SUB, :] for part, c in spots],
            [middle[part, c, own_at, :] for part, c in spots],
        )

    def gradient(corr, weights):
        keep = (iota(corr.shape, 0) & (SUB - 1)) == (iota(corr.shape, 1) & (SUB - 1))
        kept = jnp.where(keep, corr[...], 0.0)
        many = corr.shape[0] // SUB
        kept = jnp.sum(kept.reshape(many, SUB, tall), 1)
        widen = (tall, LANES)
        begin = iota(widen, 0)
        least = (iota(widen, 1) // PAD) * SUB
        to_lane = ((begin >= least) & (begin < least + SUB)).astype(F32)
        return jnp.sum(exact(kept, to_lane) * weights[0:many, :], 0, keepdims=True)

    sums = gradient(corr_first, mats_turned) + gradient(corr_second, slots_turned)
    partial[...] = jnp.broadcast_to(sums * (1.0 / width), (SUB, LANES))
    tier_copies = [
        pltpu.make_async_remote_copy(
            src_ref=partial,
            dst_ref=by_tier.at[me],
            send_sem=tier_send.at[d],
            recv_sem=tier_land.at[d],
            device_id=device,
            device_id_type=MESH,
        )
        for d, device in enumerate(tier_peers)
    ]
    for one in tier_copies:
        one.start()
    by_tier[me] = partial[...]

    own_base = last_group * count
    mat_copies = []
    for k in range(PIECES):

        def take(part, c):
            return middle[part, starts[k] // SUB + c, 0 : slots * SUB, :]

        def own_take(part, c):
            own = middle[part, starts[k] // SUB + c, own_at, :].astype(F32)
            return own.reshape(count, SUB, width)

        mix(mix_second[...], KINDS - 1, take, own_take, k, count)

        def finish(value):
            for n in range(count):
                for part in range(2):
                    out_ref[n, part] = 0.25 * value(n, part)

        apply(k, 0, own_base, 0.0, finish if k == PIECES - 1 else None)
        if k == 1:
            for one in tier_copies:
                one.wait()
            subtotal[...] = jnp.sum(by_tier[...], 0)
            by_mat[mat] = subtotal[...]
            mat_copies = [
                pltpu.make_async_remote_copy(
                    src_ref=subtotal,
                    dst_ref=by_mat.at[mat],
                    send_sem=mat_send.at[d],
                    recv_sem=mat_land.at[d],
                    device_id=device,
                    device_id_type=MESH,
                )
                for d, device in enumerate(mat_peers)
            ]
            for one in mat_copies:
                one.start()

    for one in mat_copies:
        one.wait()
    by_lane = jnp.sum(by_mat[...], 0)[0:1, :]
    grad_ref[...] = sum(by_lane[:, n * PAD : n * PAD + modes] for n in range(count))
    for one, cond in sent:
        when(cond, one.wait_send)


def per_device(
    tiers,
    mats,
    costate,
    hamiltonian,
    couplers,
    damping,
    coupling,
    levels,
    neighbour_slot,
    neighbour_mode,
    neighbour_flag,
    send_index,
):
    count, _, width, _ = costate.shape
    modes = levels.shape[1]
    slots = send_index.shape[1]
    cap = slots // tiers
    total = tiers * count
    targets = slots + count
    groups = targets // count
    batch = max(b for b in range(1, 6) if groups % b == 0) * count
    sizes = [share * width // sum(SHARES) for share in SHARES]
    tall = count * SUB
    cols = 2
    while cols * cols * 2 < tiers:
        cols *= 2
    vmem = pl.BlockSpec(memory_space=pltpu.VMEM)
    dma = pltpu.SemaphoreType.DMA

    def small(*lead):
        return pltpu.VMEM(lead + (SUB, LANES), F32)

    increment, grads = pl.pallas_call(
        functools.partial(kernel, tiers, mats),
        out_shape=(
            jax.ShapeDtypeStruct(costate.shape, F32),
            jax.ShapeDtypeStruct((1, modes), F32),
        ),
        in_specs=[vmem] * 10,
        out_specs=(vmem, vmem),
        scratch_shapes=[
            pltpu.VMEM((targets, 2, width, width), F32),
            pltpu.VMEM((2, width // SUB, targets * SUB, width), BF16),
            pltpu.VMEM((batch, 2, 4 * max(sizes), width), BF16),
            pltpu.VMEM((batch, max(sizes) // SUB, 2 * SUB, 4 * width), BF16),
            pltpu.VMEM((4 * width, width), BF16),
            pltpu.VMEM((targets * KINDS * SUB, total * SUB), BF16),
            pltpu.VMEM((count * (KINDS - 1) * SUB, slots * SUB), BF16),
            pltpu.VMEM((count * PAD, LANES), F32),
            pltpu.VMEM((count * PAD, LANES), F32),
            pltpu.VMEM((count * PAD, LANES), F32),
            pltpu.VMEM((LANES, LANES), F32),
            pltpu.VMEM((LANES, LANES), F32),
            pltpu.VMEM((LANES, LANES), jnp.int32),
            pltpu.VMEM((targets, 1, width), F32),
            pltpu.VMEM((3, SUB, LANES), jnp.int32),
            pltpu.VMEM((SUB, LANES), jnp.int32),
            pltpu.VMEM((tiers, SUB, LANES), jnp.int32),
            pltpu.VMEM((tiers, cap * PAD, LANES), F32),
            pltpu.VMEM((tiers, cap * PAD, LANES), F32),
            pltpu.VMEM((total * SUB, tall), F32),
            pltpu.VMEM((slots * SUB, tall), F32),
            small(),
            small(tiers),
            small(),
            small(mats),
            dma((1 + cols, PIECES, tiers)),
            dma((PIECES, tiers)),
        ]
        + [dma((tiers - 1,))] * 6
        + [dma((mats - 1,))] * 2
        + [pltpu.VMEM((tiers, 2, size // SUB, tall, width), BF16) for size in sizes]
        + [pltpu.VMEM((width, 4 * size), BF16) for size in sizes],
        compiler_params=pltpu.CompilerParams(
            vmem_limit_bytes=60 << 20, collective_id=0, has_side_effects=True
        ),
        name="midpoint",
    )(
        costate,
        hamiltonian,
        couplers,
        damping[None, :],
        coupling,
        levels,
        neighbour_slot,
        neighbour_mode,
        neighbour_flag,
        send_index,
    )
    return increment, grads[0]


def solution(mesh):
    blocks = P(("tier", "mat"), None)
    return jax.shard_map(
        functools.partial(per_device, mesh.shape["tier"], mesh.shape["mat"]),
        mesh=mesh,
        in_specs=(P(("tier", "mat"), None, None, None), P(), P(), P(), P()) + (blocks,) * 5,
        out_specs=(P(("tier", "mat"), None, None, None), P()),
        check_vma=False,
    )
```

```python
import functools

import jax
import jax.numpy as jnp
from jax import lax
from jax.experimental import pallas as pl
from jax.experimental.pallas import tpu as pltpu
from jax.sharding import PartitionSpec as P

SHARES = (4, 4, 4, 2, 2)
DETOUR = (1, 2)
ROUNDS = ((0, 1), (2,3), (4,))
PIECES = len(SHARES)
SUB = 8
LANES = 128
KINDS = 10
PAD = 16
F32 = jnp.float32
BF16 = jnp.bfloat16
MESH = pl.DeviceIdType.MESH
HIGH = lax.Precision.HIGHEST


def iota(shape, axis):
    return lax.broadcasted_iota(jnp.int32, shape, axis)


def exact(a, b, dims=(((1,), (0,)), ((), ()))):
    return lax.dot_general(a, b, dims, precision=HIGH, preferred_element_type=F32)


TURNED = (((1,), (1,)), ((), ()))


def dot(a, b):
    return jnp.dot(a, b, preferred_element_type=F32)


def column(row):
    n = row.shape[1]
    square = (n, n)
    return jnp.sum(jnp.where(iota(square, 0) == iota(square, 1), row, 0.0), 1, keepdims=True)


def when(cond, act):
    if cond is None:
        act()
    else:
        pl.when(cond)(act)


def kernel(
    tiers,
    mats,
    state_ref,
    ham_ref,
    coup_ref,
    damping_ref,
    strength_ref,
    levels_ref,
    slot_ref,
    mode_ref,
    flag_ref,
    index_ref,
    out_ref,
    grad_ref,
    acc,
    middle,
    left_in,
    right_in,
    right_ops,
    mix_first,
    mix_second,
    slots_coef,
    slots_weight,
    mats_coef,
    mats_turned,
    slots_turned,
    place,
    decays,
    padded,
    own_index,
    all_index,
    chosen,
    tables,
    corr_first,
    corr_second,
    partial,
    by_tier,
    subtotal,
    by_mat,
    block_send,
    block_land,
    index_send,
    index_land,
    table_send,
    table_land,
    tier_send,
    tier_land,
    mat_send,
    mat_land,
    *by_piece,
):
    gathered, left_ops = by_piece[:PIECES], by_piece[PIECES:]
    count, _, width, _ = state_ref.shape
    modes = levels_ref.shape[1]
    near = slot_ref.shape[1]
    slots = index_ref.shape[1]
    cap = slots // tiers
    total = tiers * count
    sizes = [share * width // sum(SHARES) for share in SHARES]
    starts = [sum(sizes[:k]) for k in range(PIECES)]
    tall = count * SUB
    groups = (slots + count) // count
    last_group = groups - 1
    cols = 2
    while cols * cols * 2 < tiers:
        cols *= 2
    rows = tiers // cols
    detour = DETOUR if cols == 2 else ()
    batch = max(b for b in range(1, 6) if groups % b == 0) * count

    me, mat = lax.axis_index("tier"), lax.axis_index("mat")
    z, y = me // cols, lax.rem(me, cols)
    tier_peers = [(lax.rem(me + d, tiers), mat) for d in range(1, tiers)]
    mat_peers = [(me, lax.rem(mat + d, mats)) for d in range(1, mats)]

    barrier = pltpu.get_barrier_semaphore()
    for device in tier_peers + mat_peers:
        pl.semaphore_signal(barrier, inc=1, device_id=device, device_id_type=MESH)

    def relayout(k):
        @pl.loop(0, sizes[k] // (2 * SUB))
        def _(step):
            at = pl.ds(pl.multiple_of(starts[k] + step * 2 * SUB, 2 * SUB), 2 * SUB)
            for part in range(2):
                both = state_ref[:, part, at, :].astype(F32)
                for h in range(2):
                    eight = both[:, h * SUB : (h + 1) * SUB].reshape(tall, width)
                    gathered[k][me, part, step * 2 + h] = eight.astype(BF16)

    relayout(0)
    own_index[...] = jnp.full((SUB, LANES), -1, jnp.int32)
    own_index[0:1, 0:slots] = index_ref[...]
    pl.semaphore_wait(barrier, len(tier_peers) + len(mat_peers))

    below = (jnp.maximum(z - 1, 0) * cols + y, mat)
    above = (jnp.minimum(z + 1, rows - 1) * cols + y, mat)
    beside = [(z * cols + lax.rem(y + c, cols), mat) for c in range(1, cols)]
    ways = [below, above] + beside
    sides = range(2, 2 + len(beside))
    sent = []

    def copy(k, u, way):
        return pltpu.make_async_remote_copy(
            src_ref=gathered[k].at[u],
            dst_ref=gathered[k].at[u],
            send_sem=block_send.at[way, k, u],
            recv_sem=block_land.at[k, u],
            device_id=ways[way],
            device_id_type=MESH,
        )

    def go(k, u, way, cond=None):
        one = copy(k, u, way)
        sent.append((one, cond))
        when(cond, one.start)

    def got(k, u, cond=None):
        when(cond, copy(k, u, 2).wait_recv)

    def start_own(k):
        for way in sides:
            go(k, me, way)
        go(k, me, 0, z > 0)
        go(k, me, 1, z < rows - 1)

    def tier_at(row, col):
        return jnp.clip(row, 0, rows - 1) * cols + col

    def along(k, d):
        cond, u = z + d < rows, tier_at(z + d, y)
        if k in detour and d == rows - 1:
            return
        got(k, u, cond)
        go(k, u, 0, cond & (z > 0))
        for way in sides:
            go(k, u, way, cond & (z + d != rows - 1) if k in detour else cond)
        cond, u = z - d >= 0, tier_at(z - d, y)
        got(k, u, cond)
        go(k, u, 1, cond & (z < rows - 1))
        for way in sides:
            go(k, u, way, cond & (z - d != 0) if k in detour else cond)

    def across(k):
        for c in range(1, cols):
            u = z * cols + lax.rem(y + c, cols)
            got(k, u)
            if k in detour:
                go(k, u, 0, z == rows - 1)
                go(k, u, 1, z == 0)

    def around(k):
        if k in detour:
            inner = (z < rows - 1) & (z > 0)
            for row, way in ((rows - 1, 0), (0, 1)):
                got(k, tier_at(row, 1 - y), inner)
                go(k, tier_at(row, 1 - y), way, inner)

    def rest(k):
        if k in detour:
            got(k, tier_at(rows - 1, 1 - y), z == 0)
            got(k, tier_at(0, 1 - y), z == rows - 1)
            got(k, tier_at(rows - 1, y), z == 0)
            got(k, tier_at(0, y), z == rows - 1)
        for d in range(1, rows):
            for c in range(1, cols):
                col = lax.rem(y + c, cols)
                cond = z + d < rows
                if k in detour:
                    cond = cond & (z + d != rows - 1)
                got(k, tier_at(z + d, col), cond)
                cond = z - d >= 0
                if k in detour:
                    cond = cond & (z - d != 0)
                got(k, tier_at(z - d, col), cond)

    def events(number):
        if number >= len(ROUNDS):
            return []
        pieces = ROUNDS[number]

        def first():
            for k in pieces:
                along(k, 1)
                across(k)
            if number + 1 < len(ROUNDS):
                for k in ROUNDS[number + 1]:
                    start_own(k)

        def further(d):
            for k in pieces:
                along(k, d)

        def last():
            for k in pieces:
                around(k)

        return [first] + [functools.partial(further, d) for d in range(2, rows)] + [last]

    index_copies = [
        pltpu.make_async_remote_copy(
            src_ref=own_index,
            dst_ref=all_index.at[me],
            send_sem=index_send.at[d],
            recv_sem=index_land.at[d],
            device_id=device,
            device_id_type=MESH,
        )
        for d, device in enumerate(tier_peers)
    ]
    for one in index_copies:
        one.start()
    start_own(0)
    all_index[me] = own_index[...]
    relayout(1)
    start_own(1)
    for k in range(2, PIECES):
        relayout(k)

    every = [events(number) for number in range(len(ROUNDS))]

    def step_on(*order):
        for k, i in order:
            if k < len(every) and i < len(every[k]) and every[k][i] is not None:
                every[k][i]()
                every[k][i] = None

    step_on((0, 0),)

    for i, ref in enumerate((slot_ref, mode_ref, flag_ref)):
        padded[i] = jnp.full((SUB, LANES), -1, jnp.int32)
        padded[i, 0:count, 0:near] = ref[...]
    shape = (PAD, LANES)
    kind = iota(shape, 0)
    lane = iota(shape, 1)
    mode_slot = iota(shape, 0)
    strong = [column(strength_ref[i : i + 1, :]) for i in range(2)]

    def tallest(col):
        return jnp.concatenate([col, jnp.zeros((PAD - col.shape[0], 1), F32)], 0)

    strong = [tallest(v) for v in strong]
    levels = levels_ref[...].astype(F32)
    fade = jnp.sum(levels * damping_ref[...], 1, keepdims=True)
    for n in range(count):
        slot, mode, flag = (padded[i, n : n + 1, :] for i in range(3))
        hot = (mode_slot == mode).astype(F32)
        live = (flag >= 0).astype(F32)
        level = tallest(column(levels[n : n + 1, :]))
        weight = jnp.sqrt(1.0 + jnp.sum(hot * level, 0, keepdims=True)) * live
        real = jnp.sum(hot * strong[0], 0, keepdims=True) * weight
        imag = jnp.sum(hot * strong[1], 0, keepdims=True) * weight
        other = jnp.where(flag == 1, imag, -imag)
        third = jnp.zeros_like(mode)
        for k in range(modes):
            third = jnp.where(mode == k, k % 3, third)
        values = jnp.where(kind < 4, real, jnp.where(kind < 7, imag, other))
        which = jnp.where(kind < 4, kind - 1, jnp.where(kind < 7, kind - 4, kind - 7))
        values = jnp.where((which == third) & (kind >= 1) & (kind < KINDS), values, 0.0)
        slot_hot = (iota((LANES, LANES), 0) == slot).astype(F32)
        at = slice(n * PAD, (n + 1) * PAD)
        slots_coef[at, :] = exact(values, slot_hot, TURNED)
        slots_weight[at, :] = exact(hot * weight, slot_hot, TURNED)

    step_on((0, 1))
    for one in index_copies:
        one.wait()
    place[...] = jnp.full((LANES, LANES), -1, jnp.int32)
    row = iota((1, LANES), 1)
    for u in range(tiers):
        for s in range(cap):
            index = all_index[u, 0:1, :]
            index = jnp.sum(jnp.where(row == me * cap + s, index, 0), 1, keepdims=True)
            place[u * cap + s : u * cap + s + 1, :] = jnp.broadcast_to(index + u * count, (1, LANES))
    to_mat = (place[...] == iota((LANES, LANES), 1)).astype(F32)
    spread = exact(slots_coef[...], to_mat)
    for n in range(count):
        own = jnp.where((kind == 0) & (lane == me * count + n), 1.0, 0.0)
        drop = jnp.where(kind == KINDS, fade[n : n + 1, :], 0.0)
        mats_coef[n * PAD : (n + 1) * PAD, :] = spread[n * PAD : (n + 1) * PAD] + own + drop
    def turned(table):
        return jnp.concatenate([table, jnp.zeros((LANES - count * PAD, LANES), F32)], 0).T

    mats_turned[...] = turned(exact(slots_weight[...], to_mat))
    slots_turned[...] = turned(slots_weight[...])

    for t in range(tiers):
        for s in range(cap):
            index = own_index[0:1, t * cap + s : t * cap + s + 1]
            rows_of = jnp.zeros(shape, F32)
            for n in range(count):
                rows_of = jnp.where(index == n, mats_coef[n * PAD : (n + 1) * PAD, :], rows_of)
            chosen[t, s * PAD : (s + 1) * PAD, :] = rows_of
    table_copies = [
        pltpu.make_async_remote_copy(
            src_ref=chosen.at[device[0]],
            dst_ref=tables.at[me],
            send_sem=table_send.at[d],
            recv_sem=table_land.at[d],
            device_id=device,
            device_id_type=MESH,
        )
        for d, device in enumerate(tier_peers)
    ]
    for one in table_copies:
        one.start()
    tables[me] = chosen[me]
    step_on((0, 2))

    def make_operators():
        for q in range(4):
            raw = (ham_ref[...] if q == 0 else coup_ref[q - 1]).astype(F32)
            op = ((raw + raw.T) * 0.5).astype(BF16)
            right_ops[q * width : (q + 1) * width, :] = op
            acc[q, 0] = op.astype(F32)
        for k in range(PIECES):
            stack = [
                acc[q, 0, r : r + SUB, :]
                for r in range(starts[k], starts[k] + sizes[k], SUB)
                for q in range(4)
            ]
            left_ops[k][...] = jnp.concatenate(stack, 0).T.astype(BF16)

    def blow(ref, base, table, kinds, first, across_):
        deep = iota((kinds * SUB, PAD), 0)
        down = ((deep >= (iota((kinds * SUB, PAD), 1) - first) * SUB) & (deep < (iota((kinds * SUB, PAD), 1) - first + 1) * SUB)).astype(BF16)
        big = dot(down, table.astype(BF16)).astype(BF16)
        big = dot(big, across_)
        keep = (iota(big.shape, 0) & (SUB - 1)) == (iota(big.shape, 1) & (SUB - 1))
        ref[base, :] = jnp.where(keep, big, 0.0).astype(BF16)

    def widening(count_):
        wide = (LANES, count_ * SUB)
        deep = iota(wide, 0) * SUB
        return ((iota(wide, 1) >= deep) & (iota(wide, 1) < deep + SUB)).astype(BF16)

    by_slot = widening(slots)
    high = KINDS - 1
    for n in range(count):
        table = slots_coef[n * PAD : (n + 1) * PAD, :]
        at = slice(n * high * SUB, (n + 1) * high * SUB)
        for i in range(2):
            blow(mix_second.at[i], at, table, high, 1, by_slot)
            table = table - table.astype(BF16).astype(F32)
    corr_first[...] = jnp.zeros(corr_first.shape, F32)
    corr_second[...] = jnp.zeros(corr_second.shape, F32)

    step_on((0, 3))
    make_operators()
    for one in table_copies:
        one.wait()
    by_matrix = widening(total)
    deep = KINDS * SUB

    @pl.loop(0, tiers)
    def _(u):
        for s in range(cap):
            table = tables[u, s * PAD : (s + 1) * PAD, :]
            base = pl.ds(pl.multiple_of((u * cap + s) * deep, 2 * SUB), deep)
            blow(mix_first, base, table, KINDS, 0, by_matrix)
            decays[u * cap + s] = jnp.broadcast_to(table[KINDS : KINDS + 1, 0:1], (1, width))

    step_on((1, 0))
    for n in range(count):
        table = mats_coef[n * PAD : (n + 1) * PAD, :]
        blow(mix_first, pl.ds((slots + n) * deep, deep), table, KINDS, 0, by_matrix)
        decays[slots + n] = jnp.broadcast_to(table[KINDS : KINDS + 1, 0:1], (1, width))

    def mix(coef, kinds, take, own_take, k, many):
        @pl.loop(0, sizes[k] // SUB, unroll=4)
        def _(c):
            real, imag = (
                sum(dot(a, x) for a, x in zip(coef, take(part, c))).reshape(many, kinds, SUB, width)
                for part in range(2)
            )
            a = kinds - 9
            lefts_at = pl.ds(pl.multiple_of(c * 4 * SUB, 4 * SUB), 4 * SUB)
            for t in range(many):
                if own_take is None:
                    x = real[t, 0], imag[t, 0]
                else:
                    x = own_take(0, c)[t], own_take(1, c)[t]
                p, r = real[t, a:], imag[t, a:]
                lefts = [[-x[1]], [x[0]]]
                rights = [[-x[1], x[0]]]
                for q in range(3):
                    lefts[0].append(p[q] - r[3 + q])
                    lefts[1].append(r[q] + p[3 + q])
                    rights.append([p[q] - r[6 + q], r[q] + p[6 + q]])
                for part in range(2):
                    left_in[t, part, lefts_at, :] = jnp.concatenate(lefts[part], 0).astype(BF16)
                for q in range(4):
                    at = slice(q * width, (q + 1) * width)
                    right_in[t, c, :, at] = jnp.concatenate(rights[q], 0).astype(BF16)

    def apply(k, slot0, base, scale, finish):
        at = slice(starts[k], starts[k] + sizes[k])
        chunks = sizes[k] // SUB

        def products(n, part):
            return dot(left_ops[k][...], left_in[slot0 + n, part, 0 : 4 * sizes[k], :])

        def local():
            rows_in = right_in[pl.ds(slot0, count), 0:chunks]
            back = dot(rows_in.reshape(count * chunks * 2 * SUB, 4 * width), right_ops[...])
            back = back.reshape(count, chunks, 2, SUB, width)
            for n in range(count):
                keep = scale - decays[base + n]
                for part in range(2):
                    x = left_in[slot0 + n, 1 - part, 0 : 4 * sizes[k], :].astype(F32)
                    x = x.reshape(chunks, 4, SUB, width)[:, 0].reshape(sizes[k], width)
                    x = x if part == 0 else -x
                    acc[base + n, part, at, :] += keep * x - back[n, :, part].reshape(sizes[k], width)

        if k > 0:
            local()
        if finish is None:
            for n in range(count):
                for part in range(2):
                    if k == 0:
                        acc[base + n, part] = products(n, part)
                    else:
                        acc[base + n, part] += products(n, part)
        else:
            finish(lambda n, part: acc[base + n, part] + products(n, part))
        if k == 0:
            local()

    def first_mix(k, b):
        def take(part, c):
            return [gathered[k][:, part, c].reshape(total * SUB, width)]

        mix([mix_first[b * batch * deep : (b + 1) * batch * deep, :]], KINDS, take, None, k, batch)

    def first_apply(k, b):
        @pl.loop(0, batch // count, unroll=True)
        def _(i):
            g = b * (batch // count) + i

            def finish(value):
                for part in range(2):
                    for n in range(0, count, 2):
                        pair = [
                            (0.125 * value(n + j, part)).reshape(width // SUB, SUB, width)
                            for j in range(2)
                        ]
                        at = pl.ds(pl.multiple_of(g * tall + n * SUB, 2 * SUB), 2 * SUB)
                        middle[part, :, at, :] = jnp.concatenate(pair, 1).astype(BF16)

            apply(k, i * count, g * count, 1 / 0.125, finish if k == PIECES - 1 else None)

    def correlate(target, rows_of, own_of):
        target[...] += lax.dot_general(
            jnp.concatenate(rows_of, 1),
            jnp.concatenate(own_of, 1),
            TURNED,
            preferred_element_type=F32,
        )

    def correlate_first(k):
        @pl.loop(0, sizes[k] // (2 * SUB))
        def _(step):
            spots = [(part, step * 2 + h) for part in range(2) for h in range(2)]
            correlate(
                corr_first,
                [gathered[k][:, part, c].reshape(total * SUB, width) for part, c in spots],
                [gathered[k][me, part, c] for part, c in spots],
            )

    for number, pieces in enumerate(ROUNDS):
        step_on(*((number, i) for i in range(rows + 1)), (number + 1, 0))
        todo = [(number + 1, i) for i in range(1, rows + 1)]
        for k in pieces:
            rest(k)
        for k in pieces:
            correlate_first(k)
            for b in range(groups * count // batch):
                first_mix(k, b)
                step_on(*todo[:1])
                first_apply(k, b)
                step_on(*todo[1:2])
                todo = todo[2:]
        step_on(*todo)

    own_at = slice(slots * SUB, slots * SUB + tall)

    @pl.loop(0, width // (2 * SUB))
    def _(step):
        spots = [(part, step * 2 + h) for part in range(2) for h in range(2)]
        correlate(
            corr_second,
            [middle[part, c, 0 : slots * SUB, :] for part, c in spots],
            [middle[part, c, own_at, :] for part, c in spots],
        )

    def gradient(corr, weights):
        keep = (iota(corr.shape, 0) & (SUB - 1)) == (iota(corr.shape, 1) & (SUB - 1))
        kept = jnp.where(keep, corr[...], 0.0)
        many = corr.shape[0] // SUB
        kept = jnp.sum(kept.reshape(many, SUB, tall), 1)
        widen = (tall, LANES)
        begin = iota(widen, 0)
        least = (iota(widen, 1) // PAD) * SUB
        to_lane = ((begin >= least) & (begin < least + SUB)).astype(F32)
        return jnp.sum(exact(kept, to_lane) * weights[0:many, :], 0, keepdims=True)

    sums = gradient(corr_first, mats_turned) + gradient(corr_second, slots_turned)
    partial[...] = jnp.broadcast_to(sums * (1.0 / width), (SUB, LANES))
    tier_copies = [
        pltpu.make_async_remote_copy(
            src_ref=partial,
            dst_ref=by_tier.at[me],
            send_sem=tier_send.at[d],
            recv_sem=tier_land.at[d],
            device_id=device,
            device_id_type=MESH,
        )
        for d, device in enumerate(tier_peers)
    ]
    for one in tier_copies:
        one.start()
    by_tier[me] = partial[...]

    own_base = last_group * count
    mat_copies = []
    for k in range(PIECES):

        def take(part, c):
            return [middle[part, starts[k] // SUB + c, 0 : slots * SUB, :]] * 2

        def own_take(part, c):
            own = middle[part, starts[k] // SUB + c, own_at, :].astype(F32)
            return own.reshape(count, SUB, width)

        mix([mix_second[0], mix_second[1]], KINDS - 1, take, own_take, k, count)

        def finish(value):
            for n in range(count):
                for part in range(2):
                    out_ref[n, part] = 0.25 * value(n, part)

        apply(k, 0, own_base, 0.0, finish if k == PIECES - 1 else None)
        if k == 1:
            for one in tier_copies:
                one.wait()
            subtotal[...] = jnp.sum(by_tier[...], 0)
            by_mat[mat] = subtotal[...]
            mat_copies = [
                pltpu.make_async_remote_copy(
                    src_ref=subtotal,
                    dst_ref=by_mat.at[mat],
                    send_sem=mat_send.at[d],
                    recv_sem=mat_land.at[d],
                    device_id=device,
                    device_id_type=MESH,
                )
                for d, device in enumerate(mat_peers)
            ]
            for one in mat_copies:
                one.start()

    for one in mat_copies:
        one.wait()
    by_lane = jnp.sum(by_mat[...], 0)[0:1, :]
    grad_ref[...] = sum(by_lane[:, n * PAD : n * PAD + modes] for n in range(count))
    for one, cond in sent:
        when(cond, one.wait_send)


def per_device(
    tiers,
    mats,
    costate,
    hamiltonian,
    couplers,
    damping,
    coupling,
    levels,
    neighbour_slot,
    neighbour_mode,
    neighbour_flag,
    send_index,
):
    count, _, width, _ = costate.shape
    modes = levels.shape[1]
    slots = send_index.shape[1]
    cap = slots // tiers
    total = tiers * count
    targets = slots + count
    groups = targets // count
    batch = max(b for b in range(1, 6) if groups % b == 0) * count
    sizes = [share * width // sum(SHARES) for share in SHARES]
    tall = count * SUB
    cols = 2
    while cols * cols * 2 < tiers:
        cols *= 2
    vmem = pl.BlockSpec(memory_space=pltpu.VMEM)
    dma = pltpu.SemaphoreType.DMA

    def small(*lead):
        return pltpu.VMEM(lead + (SUB, LANES), F32)

    increment, grads = pl.pallas_call(
        functools.partial(kernel, tiers, mats),
        out_shape=(
            jax.ShapeDtypeStruct(costate.shape, F32),
            jax.ShapeDtypeStruct((1, modes), F32),
        ),
        in_specs=[vmem] * 10,
        out_specs=(vmem, vmem),
        scratch_shapes=[
            pltpu.VMEM((targets, 2, width, width), F32),
            pltpu.VMEM((2, width // SUB, targets * SUB, width), BF16),
            pltpu.VMEM((batch, 2, 4 * max(sizes), width), BF16),
            pltpu.VMEM((batch, max(sizes) // SUB, 2 * SUB, 4 * width), BF16),
            pltpu.VMEM((4 * width, width), BF16),
            pltpu.VMEM((targets * KINDS * SUB, total * SUB), BF16),
            pltpu.VMEM((2, count * (KINDS - 1) * SUB, slots * SUB), BF16),
            pltpu.VMEM((count * PAD, LANES), F32),
            pltpu.VMEM((count * PAD, LANES), F32),
            pltpu.VMEM((count * PAD, LANES), F32),
            pltpu.VMEM((LANES, LANES), F32),
            pltpu.VMEM((LANES, LANES), F32),
            pltpu.VMEM((LANES, LANES), jnp.int32),
            pltpu.VMEM((targets, 1, width), F32),
            pltpu.VMEM((3, SUB, LANES), jnp.int32),
            pltpu.VMEM((SUB, LANES), jnp.int32),
            pltpu.VMEM((tiers, SUB, LANES), jnp.int32),
            pltpu.VMEM((tiers, cap * PAD, LANES), F32),
            pltpu.VMEM((tiers, cap * PAD, LANES), F32),
            pltpu.VMEM((total * SUB, tall), F32),
            pltpu.VMEM((slots * SUB, tall), F32),
            small(),
            small(tiers),
            small(),
            small(mats),
            dma((1 + cols, PIECES, tiers)),
            dma((PIECES, tiers)),
        ]
        + [dma((tiers - 1,))] * 6
        + [dma((mats - 1,))] * 2
        + [pltpu.VMEM((tiers, 2, size // SUB, tall, width), BF16) for size in sizes]
        + [pltpu.VMEM((width, 4 * size), BF16) for size in sizes],
        compiler_params=pltpu.CompilerParams(
            vmem_limit_bytes=60 << 20, collective_id=0, has_side_effects=True
        ),
        name="midpoint",
    )(
        costate,
        hamiltonian,
        couplers,
        damping[None, :],
        coupling,
        levels,
        neighbour_slot,
        neighbour_mode,
        neighbour_flag,
        send_index,
    )
    return increment, grads[0]


def solution(mesh):
    blocks = P(("tier", "mat"), None)
    return jax.shard_map(
        functools.partial(per_device, mesh.shape["tier"], mesh.shape["mat"]),
        mesh=mesh,
        in_specs=(P(("tier", "mat"), None, None, None), P(), P(), P(), P()) + (blocks,) * 5,
        out_specs=(P(("tier", "mat"), None, None, None), P()),
        check_vma=False,
    )
```
